32 devices in a mesh: seq: 16 (over z, y, core), wgt: 2 (over x).
Axes of the slice: x: 2, y: 2, z: 4, core: 2. Of those that a mesh axis runs over, the one named last changes fastest.
Arguments:
- hidden: bfloat16 [6144, 5376], P('seq', 'wgt'), may hold values from -6 to 6
- q_weight: bfloat16 [2, 5376, 2048], P(None, 'seq', 'wgt'), may hold values from -448 to 448, as said below
- k_weight: bfloat16 [2, 5376, 1024], P(None, 'seq', 'wgt'), may hold values from -448 to 448, as said below
- v_weight: bfloat16 [2, 5376, 1024], P(None, 'seq', 'wgt'), may hold values from -448 to 448, as said below
- o_weight: bfloat16 [2, 2048, 5376], P(None, 'seq', 'wgt'), may hold values from -448 to 448, as said below
- q_scale: int32 [2, 42, 16], P(None, None, 'wgt'), may hold values from 113 to 117
- k_scale: int32 [2, 42, 8], P(None, None, 'wgt'), may hold values from 113 to 117
- v_scale: int32 [2, 42, 8], P(None, None, 'wgt'), may hold values from 113 to 117
- o_scale: int32 [2, 16, 42], replicated, may hold values from 113 to 117
- in_gain: float32 [2, 5376], replicated, may hold values from 0.5 to 1.5
- post_gain: float32 [2, 5376], P(None, 'wgt'), may hold values from 0.5 to 1.5
- q_gain: float32 [2, 128], replicated, may hold values from 0.1 to 1.9
- k_gain: float32 [2, 128], replicated, may hold values from 0.1 to 1.9
- windows: int32 [2], replicated, may hold values from 512 to 1024, as said below
Outputs:
- state: bfloat16 [6144, 5376], P('seq', 'wgt')
The draws below stay inside these ranges and needn't reach their ends.
Inputs may be any that keep to these rules, and one draw needn't show every extreme that they name: `q_weight`: every entry is a finite value of the e4m3 floating-point format: sign, 3 mantissa bits, exponents of that format. `k_weight`: every entry is a finite value of the e4m3 floating-point format. `v_weight`: every entry is a finite value of the e4m3 floating-point format. `o_weight`: every entry is a finite value of the e4m3 floating-point format. `windows`: one layer's window is exactly 1024.
All inputs are finite; a program needn't handle non-finite values.
Results may differ from the reference program's by a relative error of at most 0.0095.
Values may be sent and summed in bfloat16 or wider, within the bound.
No kernel may reach another device: no remote copies, remote signals or barrier semaphores. Data moves between devices by JAX's collectives and lax.ppermute only.
A program may use at most 192 MiB of HBM per device.

```python
import jax
import jax.numpy as jnp
from jax import lax

D = 5376
HEADS = 16
KV_HEADS = 8
HD = 128
BLOCK = 128
WINDOW = 1024
LAYERS = 2
TOK_DEV = 384
TOKENS = 6144
HALO = 3


def e4m3_values(key, shape):
    sign_key, expo_key, mant_key = jax.random.split(key, 3)
    sign = jax.random.randint(sign_key, shape, 0, 2)
    expo = jax.random.randint(expo_key, shape, 4, 15)
    mant = jax.random.randint(mant_key, shape, 0, 8)
    value = (1.0 - 2.0 * sign.astype(jnp.float32)) * (1.0 + mant.astype(jnp.float32) / 8.0) * jnp.exp2(expo.astype(jnp.float32) - 7.0)
    return value.astype(jnp.bfloat16)


def draw_q_weight(key, part):
    return e4m3_values(jax.random.fold_in(key, 11), (LAYERS, D, HEADS * HD))


def draw_k_weight(key, part):
    return e4m3_values(jax.random.fold_in(key, 12), (LAYERS, D, KV_HEADS * HD))


def draw_v_weight(key, part):
    return e4m3_values(jax.random.fold_in(key, 13), (LAYERS, D, KV_HEADS * HD))


def draw_o_weight(key, part):
    return e4m3_values(jax.random.fold_in(key, 14), (LAYERS, HEADS * HD, D))


def draw_windows(key, part):
    length_key = jax.random.fold_in(key, 21)
    pick_key = jax.random.fold_in(key, 22)
    lengths = jax.random.randint(length_key, (LAYERS,), WINDOW // 2, WINDOW + 1)
    chosen = jax.random.randint(pick_key, (), 0, LAYERS)
    layer_ids = jnp.arange(LAYERS, dtype=jnp.int32)
    return jnp.where(layer_ids == chosen, WINDOW, lengths).astype(jnp.int32)


def set_ends(array, own_key, smallest, largest):
    longest = array.shape.index(max(array.shape))
    spots = []
    for shift in (0, 1):
        where = [jax.random.randint(jax.random.fold_in(own_key, axis), (), 0, length) for axis, length in enumerate(array.shape)]
        where[longest] = (where[longest] + shift) % array.shape[longest]
        spots.append(tuple(where))
    return array.at[spots[0]].set(smallest).at[spots[1]].set(largest)


def level_of(stream_key, shape, shards, low, top_value):
    loudness = 1.0
    for axis_at, shards_of in shards:
        steps = jax.random.uniform(jax.random.fold_in(jax.random.fold_in(stream_key, 6), axis_at), (shards_of,), jnp.float32, low / len(shards), top_value / len(shards))
        loudness = loudness * jnp.repeat(jnp.exp(steps), shape[axis_at] // shards_of).reshape((-1,) + (1,) * (len(shape) - 1 - axis_at))
    return loudness


def noise(own_key, shape, spread, most, pieces=(), kind=jnp.bfloat16):
    drawn = spread * jax.random.normal(own_key, shape, jnp.float32)
    if pieces:
        drawn = drawn * level_of(own_key, shape, pieces, -0.22, 0.18)
    return jnp.clip(drawn, -most, most).astype(kind)


def setup_inputs(seed: int = 0) -> dict:
    key_list = jax.random.split(jax.random.key(seed), 15)
    hidden = noise(key_list[0], (TOKENS, D), 1.0, 6.0, ((0, 16), (1, 2)))
    q_weight = draw_q_weight(jax.random.fold_in(key_list[14], 71), 0)
    k_weight = draw_k_weight(jax.random.fold_in(key_list[14], 71), 0)
    v_weight = draw_v_weight(jax.random.fold_in(key_list[14], 71), 0)
    o_weight = draw_o_weight(jax.random.fold_in(key_list[14], 71), 0)
    q_scale = set_ends(jax.random.randint(key_list[5], (LAYERS, D // BLOCK, HEADS * HD // BLOCK), 113, 118), jax.random.fold_in(key_list[5], 1), 113, 117).astype(jnp.int32)
    k_scale = set_ends(jax.random.randint(key_list[6], (LAYERS, D // BLOCK, KV_HEADS * HD // BLOCK), 113, 118), jax.random.fold_in(key_list[6], 1), 113, 117).astype(jnp.int32)
    v_scale = set_ends(jax.random.randint(key_list[7], (LAYERS, D // BLOCK, KV_HEADS * HD // BLOCK), 113, 118), jax.random.fold_in(key_list[7], 1), 113, 117).astype(jnp.int32)
    o_scale = set_ends(jax.random.randint(key_list[8], (LAYERS, HEADS * HD // BLOCK, D // BLOCK), 113, 118), jax.random.fold_in(key_list[8], 1), 113, 117).astype(jnp.int32)
    in_gain = jnp.clip(1.0 + 0.1 * jax.random.normal(key_list[9], (LAYERS, D), jnp.float32), 0.5, 1.5)
    post_gain = jnp.clip(1.0 + 0.1 * jax.random.normal(key_list[10], (LAYERS, D), jnp.float32), 0.5, 1.5)
    q_gain = jnp.clip(1.0 + 0.18 * jax.random.normal(key_list[11], (LAYERS, HD), jnp.float32), 0.1, 1.9)
    k_gain = jnp.clip(1.0 + 0.18 * jax.random.normal(key_list[12], (LAYERS, HD), jnp.float32), 0.1, 1.9)
    windows = draw_windows(jax.random.fold_in(key_list[14], 71), 0)
    return dict(hidden=hidden, q_weight=q_weight, k_weight=k_weight, v_weight=v_weight, o_weight=o_weight, q_scale=q_scale, k_scale=k_scale, v_scale=v_scale, o_scale=o_scale, in_gain=in_gain, post_gain=post_gain, q_gain=q_gain, k_gain=k_gain, windows=windows)


eps = 1e-06
query_scale = 168.0 ** (-0.5)
rope_base = 10000.0

def rmsnorm(values, gain):
    return values * lax.rsqrt(lax.optimization_barrier(jnp.mean(values * values, axis=-1, keepdims=True)) + eps) * gain.astype(jnp.float32)

def rotate(values, position):
    half = values.shape[-1] // 2
    inverse = rope_base ** (-jnp.arange(half, dtype=jnp.float32) * 2.0 / values.shape[-1])
    angles = position.astype(jnp.float32)[:, None] * inverse[None, :]
    cosine = jnp.cos(angles)[:, None, :]
    sine = jnp.sin(angles)[:, None, :]
    first = values[..., :half]
    second = values[..., half:]
    return jnp.concatenate([first * cosine - second * sine, second * cosine + first * sine], axis=-1)

def dequantize(codes, scale_codes):
    factor = jnp.exp2(scale_codes.astype(jnp.float32) - 127.0)
    factor = jnp.repeat(jnp.repeat(factor, BLOCK, axis=0), BLOCK, axis=1)
    return (codes.astype(jnp.float32) * factor).astype(jnp.bfloat16)

def attend(queries, key_rows, value_rows, window):
    span = TOK_DEV
    reach = HALO * TOK_DEV
    groups = HEADS // KV_HEADS
    key_padded = jnp.pad(key_rows, ((reach, 0), (0, 0), (0, 0)))
    value_padded = jnp.pad(value_rows, ((reach, 0), (0, 0), (0, 0)))

    def one_block(index):
        begin = (index * span).astype(jnp.int32)
        query_block = lax.dynamic_slice_in_dim(queries, begin, span, 0).reshape(span, KV_HEADS, groups, HD).astype(jnp.float32)
        key_block = lax.dynamic_slice_in_dim(key_padded, begin, reach + span, 0).astype(jnp.float32)
        value_block = lax.dynamic_slice_in_dim(value_padded, begin, reach + span, 0).astype(jnp.float32)
        scores = jnp.einsum('qkgd,skd->kgqs', query_block, key_block)
        query_pos = begin + jnp.arange(span, dtype=jnp.int32)
        key_pos = begin - reach + jnp.arange(reach + span, dtype=jnp.int32)
        gap = query_pos[:, None] - key_pos[None, :]
        allowed = (key_pos[None, :] >= 0) & (gap >= 0) & (gap < window)
        scores = jnp.where(allowed, scores, -1e+30)
        top = lax.optimization_barrier(jnp.max(scores, axis=-1, keepdims=True))
        expval = jnp.exp(scores - top)
        weights = (expval / lax.optimization_barrier(jnp.sum(expval, axis=-1, keepdims=True))).astype(jnp.bfloat16)
        mixed = jnp.einsum('kgqs,skd->qkgd', weights.astype(jnp.float32), value_block)
        return mixed.reshape(span, HEADS * HD).astype(jnp.bfloat16)
    blocks = lax.map(one_block, jnp.arange(TOKENS // TOK_DEV, dtype=jnp.int32))
    return blocks.reshape(TOKENS, HEADS * HD)

def reference(hidden, q_weight, k_weight, v_weight, o_weight, q_scale, k_scale, v_scale, o_scale, in_gain, post_gain, q_gain, k_gain, windows):
    position = jnp.arange(TOKENS, dtype=jnp.int32)
    state = hidden
    for layer_idx in range(LAYERS):
        normed = rmsnorm(state.astype(jnp.float32), in_gain[layer_idx]).astype(jnp.bfloat16)
        queries = jnp.dot(normed, dequantize(q_weight[layer_idx], q_scale[layer_idx]), preferred_element_type=jnp.float32)
        key_rows = jnp.dot(normed, dequantize(k_weight[layer_idx], k_scale[layer_idx]), preferred_element_type=jnp.float32)
        value_rows = jnp.dot(normed, dequantize(v_weight[layer_idx], v_scale[layer_idx]), preferred_element_type=jnp.float32)
        queries = (rotate(rmsnorm(queries.reshape(TOKENS, HEADS, HD), q_gain[layer_idx]), position) * query_scale).astype(jnp.bfloat16)
        key_rows = rotate(rmsnorm(key_rows.reshape(TOKENS, KV_HEADS, HD), k_gain[layer_idx]), position).astype(jnp.bfloat16)
        value_rows = value_rows.reshape(TOKENS, KV_HEADS, HD).astype(jnp.bfloat16)
        mixed = attend(queries, key_rows, value_rows, windows[layer_idx])
        projected = jnp.dot(mixed, dequantize(o_weight[layer_idx], o_scale[layer_idx]), preferred_element_type=jnp.float32)
        state = (state.astype(jnp.float32) + rmsnorm(projected, post_gain[layer_idx])).astype(jnp.bfloat16)
    return state
```

```python
import functools

import jax
import jax.numpy as jnp
from jax import lax
from jax.experimental import pallas as pl
from jax.experimental.pallas import tpu as pltpu
from jax.sharding import PartitionSpec as P

HD = 128
BLOCK = 128
WINDOW = 1024
LAYERS = 2


eps = 1e-06
query_scale = 168.0 ** (-0.5)
rope_base = 10000.0


def passed_along(array, axis, by):
    size = lax.axis_size(axis)
    pairs = [(i, i + by) for i in range(size) if 0 <= i + by < size]
    return lax.ppermute(array, axis, pairs)


def rmsnorm(values, gain):
    return values * lax.rsqrt(jnp.mean(values * values, axis=-1, keepdims=True) + eps) * gain


def rotate(values, position):
    half = values.shape[-1] // 2
    inverse = rope_base ** (-jnp.arange(half, dtype=jnp.float32) * 2.0 / values.shape[-1])
    angles = position.astype(jnp.float32)[:, None] * inverse[None, :]
    cosine = jnp.cos(angles)[:, None, :]
    sine = jnp.sin(angles)[:, None, :]
    first = values[..., :half]
    second = values[..., half:]
    return jnp.concatenate(
        [first * cosine - second * sine, second * cosine + first * sine], axis=-1
    )


def expand_scales(scale_codes):
    factor = jnp.exp2(scale_codes.astype(jnp.float32) - 127.0)
    return jnp.repeat(jnp.repeat(factor, BLOCK, axis=0), BLOCK, axis=1).astype(jnp.bfloat16)


def per_device_plain(
    hidden,
    q_weight,
    k_weight,
    v_weight,
    o_weight,
    q_scale,
    k_scale,
    v_scale,
    o_scale,
    in_gain,
    post_gain,
    q_gain,
    k_gain,
    windows,
):
    local_rows = hidden.shape[0]
    width_share = hidden.shape[1]
    model_width = in_gain.shape[1]
    seq_index = lax.axis_index("seq")
    column_offset = lax.axis_index("wgt") * width_share
    halo_count = -(-(WINDOW - 1) // local_rows)
    position = seq_index * local_rows + jnp.arange(local_rows, dtype=jnp.int32)
    key_position = (
        seq_index * local_rows
        - halo_count * local_rows
        + jnp.arange((halo_count + 1) * local_rows, dtype=jnp.int32)
    )
    gap = position[:, None] - key_position[None, :]
    columns = column_offset + jnp.arange(width_share, dtype=jnp.int32)
    pick = (
        (columns // BLOCK)[None, :] == jnp.arange(model_width // BLOCK, dtype=jnp.int32)[:, None]
    ).astype(jnp.float32)
    gathered = (
        lax.all_gather(q_weight, "seq", axis=1, tiled=True),
        lax.all_gather(k_weight, "seq", axis=1, tiled=True),
        lax.all_gather(v_weight, "seq", axis=1, tiled=True),
        lax.all_gather(o_weight, "seq", axis=1, tiled=True),
    )
    state = hidden
    for layer_idx in range(LAYERS):
        outgoing = state
        arriving = lax.all_gather(outgoing, "wgt", axis=1, tiled=True)
        normed = rmsnorm(arriving.astype(jnp.float32), in_gain[layer_idx]).astype(jnp.bfloat16)
        tables = (
            expand_scales(q_scale[layer_idx]),
            expand_scales(k_scale[layer_idx]),
            expand_scales(v_scale[layer_idx]),
        )
        o_factor = jnp.exp2(o_scale[layer_idx].astype(jnp.float32) - 127.0)
        o_columns = jnp.dot(o_factor, pick, precision=lax.Precision.HIGHEST)
        o_table = jnp.repeat(o_columns, BLOCK, axis=0).astype(jnp.bfloat16)
        queries = jnp.dot(
            normed, gathered[0][layer_idx] * tables[0], preferred_element_type=jnp.float32
        )
        key_part = jnp.dot(
            normed, gathered[1][layer_idx] * tables[1], preferred_element_type=jnp.float32
        )
        value_part = jnp.dot(
            normed, gathered[2][layer_idx] * tables[2], preferred_element_type=jnp.float32
        )
        queries = (
            rotate(rmsnorm(queries.reshape(local_rows, -1, HD), q_gain[layer_idx]), position)
            * query_scale
        ).astype(jnp.bfloat16)
        key_heads = rotate(
            rmsnorm(key_part.reshape(local_rows, -1, HD), k_gain[layer_idx]), position
        ).astype(jnp.bfloat16)
        key_flat = key_heads.reshape(local_rows, -1)
        value_flat = value_part.astype(jnp.bfloat16)
        earlier = []
        for distance in range(1, halo_count + 1):
            earlier.insert(0, passed_along((key_flat, value_flat), "seq", distance))
        kv_local = key_flat.shape[1] // HD
        groups = queries.shape[1] // kv_local
        all_keys = jnp.concatenate([item[0] for item in earlier] + [key_flat], axis=0).reshape(
            -1, kv_local, HD
        )
        all_values = jnp.concatenate([item[1] for item in earlier] + [value_flat], axis=0).reshape(
            -1, kv_local, HD
        )
        grouped = queries.reshape(local_rows, kv_local, groups, HD)
        scores = jnp.einsum("qkgd,skd->kgqs", grouped, all_keys, preferred_element_type=jnp.float32)
        allowed = (key_position[None, :] >= 0) & (gap >= 0) & (gap < windows[layer_idx])
        scores = jnp.where(allowed, scores, -1e30)
        top = jnp.max(scores, axis=-1, keepdims=True)
        expval = jnp.exp(scores - top)
        weights = (expval / jnp.sum(expval, axis=-1, keepdims=True)).astype(jnp.bfloat16)
        mixed = jnp.einsum(
            "kgqs,skd->qkgd", weights, all_values, preferred_element_type=jnp.float32
        )
        mixed = mixed.reshape(local_rows, -1).astype(jnp.bfloat16)
        mixed_full = lax.all_gather(mixed, "wgt", axis=1, tiled=True)
        projected = jnp.dot(
            mixed_full, gathered[3][layer_idx] * o_table, preferred_element_type=jnp.float32
        )
        post_squares = lax.psum(jnp.sum(projected * projected, axis=-1), "wgt")
        post = (
            projected
            * lax.rsqrt(post_squares / model_width + eps)[:, None]
            * post_gain[layer_idx][None, :]
        )
        state = (state.astype(jnp.float32) + post).astype(jnp.bfloat16)
    return state


def gated(array, after):
    if after is None:
        return array
    return lax.optimization_barrier((array, after))[0]


def ring_pairs(chips):
    walk = [0] + list(range(1, chips, 2)) + list(range(chips - 2, 0, -2))
    hops = [(walk[i], walk[(i + 1) % chips]) for i in range(chips)]
    forward = [(2 * a + core, 2 * b + core) for a, b in hops for core in range(2)]
    return walk, forward, [(b, a) for a, b in forward]


def ring_gather(block, chips, after, holds=()):
    _, forward, backward = ring_pairs(chips)
    back = ahead = gated(block, after)
    steps = []
    for hop in range(1, chips // 2):
        back = lax.ppermute(back, "seq", forward)
        ahead = lax.ppermute(ahead, "seq", backward)
        steps.append((back, ahead))
        if hop <= len(holds):
            back, ahead, _ = lax.optimization_barrier((back, ahead, holds[hop - 1]))
    half = block.shape[0] // 2
    far = (lax.ppermute(back[:half], "seq", forward), lax.ppermute(ahead[half:], "seq", backward))
    return steps, far, steps[min(1, len(steps) - 1)]


def swap_pairs(size):
    return [(i, i ^ 1) for i in range(size)]


def project_kernel(at_ref, *refs, counts, heads, scale, in_place, lead):
    parts, rest = refs[:counts], refs[counts:]
    states, rest = rest[:4], rest[4:]
    cos_ref, sin_ref, gain_ref = rest[:3]
    if lead:
        out_ref, factor_ref, weight, state, sems = rest[3:]
    else:
        factor_ref, out_ref, weight, state, sems = rest[3:]
    tokens, width = states[0].shape
    copies = []
    for i, part in enumerate(parts):
        begin = pl.multiple_of(at_ref[2 + i], 16)
        copies.append(pltpu.make_async_copy(part, weight.at[pl.ds(begin, part.shape[0])], sems.at[i]))
    for i, piece in enumerate(states):
        copies.append(pltpu.make_async_copy(piece, state.at[i], sems.at[counts + i]))
    for copy in copies:
        copy.start()
    for copy in copies[: counts + 2]:
        copy.wait()
    core, wgt = at_ref[0], at_ref[1]
    own_rows = pl.ds(pl.multiple_of(wgt * width, 128), width)
    far_rows = pl.ds(pl.multiple_of((1 - wgt) * width, 128), width)
    for t in range(2):
        if t == 1:
            for copy in copies[counts + 2 :]:
                copy.wait()
        near, far = state[2 * t], state[2 * t + 1]
        values = jnp.dot(near, weight[own_rows, :], preferred_element_type=jnp.float32)
        values = values + jnp.dot(far, weight[far_rows, :], preferred_element_type=jnp.float32)
        rows = slice(t * tokens, (t + 1) * tokens)
        if lead:
            squares = 0.0
            for piece in (near, far):
                wide = piece.astype(jnp.float32)
                squares = squares + jnp.sum(wide * wide, axis=-1, keepdims=True)
            factor = lax.rsqrt(squares / (2 * width) + eps)
            factor_ref[rows, :] = jnp.broadcast_to(factor, (tokens, HD))
        else:
            factor = factor_ref[rows, :]
        if in_place:
            begin = pl.multiple_of(jnp.bitwise_xor(core, t) * tokens, 128)
        else:
            begin = t * tokens
        for h in range(values.shape[1] // HD):
            columns = slice(h * HD, (h + 1) * HD)
            value = values[:, columns] * factor
            if h < heads:
                value = value * lax.rsqrt(jnp.mean(value * value, axis=-1, keepdims=True) + eps) * gain_ref[...]
                value = value * cos_ref[rows, :] + pltpu.roll(value, HD // 2, 1) * sin_ref[rows, :]
                if scale is not None:
                    value = value * scale
            out_ref[pl.ds(begin, tokens), columns] = value.astype(jnp.bfloat16)


def project(at, parts, states, cosine, sine, gain, factor, heads, scale, in_place):
    tokens, width = states[0].shape
    columns = parts[0].shape[1]
    lead = factor is None
    anywhere = pl.BlockSpec(memory_space=pl.ANY)
    local = pl.BlockSpec(memory_space=pltpu.VMEM)
    out = jax.ShapeDtypeStruct((2 * tokens, columns), jnp.bfloat16)
    factors = jax.ShapeDtypeStruct((2 * tokens, HD), jnp.float32)
    return pl.pallas_call(
        functools.partial(
            project_kernel, counts=len(parts), heads=heads, scale=scale, in_place=in_place, lead=lead
        ),
        in_specs=[pl.BlockSpec(memory_space=pltpu.SMEM)]
        + [anywhere] * (len(parts) + 4)
        + [local] * (3 if lead else 4),
        out_specs=[local, local] if lead else local,
        out_shape=[out, factors] if lead else out,
        scratch_shapes=[
            pltpu.VMEM((2 * width, columns), jnp.bfloat16),
            pltpu.VMEM((4, tokens, width), jnp.bfloat16),
            pltpu.SemaphoreType.DMA((len(parts) + 4,)),
        ],
        compiler_params=pltpu.CompilerParams(vmem_limit_bytes=32 * 2**20),
        cost_estimate=pl.CostEstimate(
            flops=8 * tokens * width * columns,
            bytes_accessed=8 * tokens * width + 4 * width * columns,
            transcendentals=tokens,
        ),
    )(at, *parts, *states, cosine, sine, gain, *([] if lead else [factor]))


def output_kernel(at_ref, *refs, counts):
    parts, rest = refs[:counts], refs[counts:]
    pieces, rest = rest[:4], rest[4:]
    out_ref, squares_ref, weight, mixed, sems = rest
    tokens, share = pieces[0].shape
    copies = []
    for i, piece in enumerate(pieces):
        copies.append(pltpu.make_async_copy(piece, mixed.at[at_ref[i]], sems.at[counts + i]))
    for i, part in enumerate(parts):
        begin = pl.multiple_of(at_ref[4 + i], 16)
        copies.append(pltpu.make_async_copy(part, weight.at[pl.ds(begin, part.shape[0])], sems.at[i]))
    for copy in copies:
        copy.start()
    for copy in copies:
        copy.wait()
    width = out_ref.shape[1]
    tile = next(t for t in (896, 512, 384, 256, 128) if width % t == 0)
    squares = jnp.zeros((tokens, 1), jnp.float32)
    for n in range(width // tile):
        columns = slice(n * tile, (n + 1) * tile)
        values = jnp.zeros((tokens, tile), jnp.float32)
        for p in range(4):
            values = values + jnp.dot(
                mixed[p], weight[p * share : (p + 1) * share, columns], preferred_element_type=jnp.float32
            )
        out_ref[:, columns] = values
        squares = squares + jnp.sum(values * values, axis=-1, keepdims=True)
    squares_ref[...] = jnp.broadcast_to(squares, squares_ref.shape)


def output(at, parts, pieces):
    tokens, share = pieces[0].shape
    width = parts[0].shape[1]
    anywhere = pl.BlockSpec(memory_space=pl.ANY)
    local = pl.BlockSpec(memory_space=pltpu.VMEM)
    return pl.pallas_call(
        functools.partial(output_kernel, counts=len(parts)),
        in_specs=[pl.BlockSpec(memory_space=pltpu.SMEM)] + [anywhere] * (len(parts) + 4),
        out_specs=[local, local],
        out_shape=[
            jax.ShapeDtypeStruct((tokens, width), jnp.float32),
            jax.ShapeDtypeStruct((tokens, HD), jnp.float32),
        ],
        scratch_shapes=[
            pltpu.VMEM((4 * share, width), jnp.bfloat16),
            pltpu.VMEM((4, tokens, share), jnp.bfloat16),
            pltpu.SemaphoreType.DMA((len(parts) + 4,)),
        ],
        compiler_params=pltpu.CompilerParams(vmem_limit_bytes=32 * 2**20),
        cost_estimate=pl.CostEstimate(
            flops=8 * tokens * width * share, bytes_accessed=12 * share * width, transcendentals=0
        ),
    )(at, *parts, *pieces)


def attend_kernel(place_ref, q_ref, *refs, reach):
    kv_refs, out_ref, keys_ref = refs[:-2], refs[-2], refs[-1]
    tile = q_ref.shape[0]
    rows = keys_ref.shape[0] - reach
    kv_heads = keys_ref.shape[1] // (2 * HD)
    groups = q_ref.shape[1] // (kv_heads * HD)
    step = pl.program_id(0)

    @pl.when(step == 0)
    def _():
        begin = 0
        for ref in kv_refs:
            keys_ref[begin : begin + ref.shape[0], :] = ref[...]
            begin += ref.shape[0]

    core, first, window = place_ref[0], place_ref[1], place_ref[2]
    steps = rows // (2 * tile)
    side = (step >= steps).astype(jnp.int32)
    begin = (jnp.bitwise_xor(core, side) * steps + step - side * steps) * tile
    begin = pl.multiple_of(begin, tile)
    span = reach + tile
    row = lax.broadcasted_iota(jnp.int32, (tile, span), 0)
    column = lax.broadcasted_iota(jnp.int32, (tile, span), 1)
    gap = reach + row - column
    allowed = (gap >= 0) & (gap < window) & (column >= -(first + begin))
    bias = jnp.where(allowed, 0.0, -1e30).astype(jnp.float32)
    bias = jnp.concatenate([bias] * groups, axis=0)
    for g in range(kv_heads):
        key = keys_ref[pl.ds(begin, span), g * HD : (g + 1) * HD]
        value = keys_ref[pl.ds(begin, span), (kv_heads + g) * HD : (kv_heads + g + 1) * HD]
        query = jnp.concatenate(
            [q_ref[:, (g * groups + j) * HD : (g * groups + j + 1) * HD] for j in range(groups)], axis=0
        )
        scores = lax.dot_general(query, key, (((1,), (1,)), ((), ())), preferred_element_type=jnp.float32)
        scores = scores + bias
        top = jnp.max(scores, axis=-1, keepdims=True)
        expval = jnp.exp(scores - top)
        total = jnp.sum(expval, axis=-1, keepdims=True)
        mixed = jnp.dot(expval.astype(jnp.bfloat16), value, preferred_element_type=jnp.float32)
        mixed = (mixed / total).astype(jnp.bfloat16)
        for j in range(groups):
            out_ref[:, (g * groups + j) * HD : (g * groups + j + 1) * HD] = mixed[j * tile : (j + 1) * tile]


def attend(queries, pieces, place, reach):
    rows, columns = queries.shape
    tile = 128
    width = pieces[0].shape[1]
    return pl.pallas_call(
        functools.partial(attend_kernel, reach=reach),
        grid_spec=pltpu.PrefetchScalarGridSpec(
            num_scalar_prefetch=1,
            grid=(rows // tile,),
            in_specs=[pl.BlockSpec((tile, columns), lambda i, place: (i, 0))]
            + [pl.BlockSpec(piece.shape, lambda i, place: (0, 0)) for piece in pieces],
            out_specs=pl.BlockSpec((tile, columns), lambda i, place: (i, 0)),
            scratch_shapes=[pltpu.VMEM((reach + rows, width), jnp.bfloat16)],
        ),
        out_shape=jax.ShapeDtypeStruct((rows, columns), jnp.bfloat16),
        cost_estimate=pl.CostEstimate(
            flops=4 * rows * columns * (reach + tile),
            bytes_accessed=4 * rows * columns,
            transcendentals=rows * columns // HD * (reach + tile),
        ),
    )(place, queries, *pieces)


def per_device_pairs(
    hidden,
    q_weight,
    k_weight,
    v_weight,
    o_weight,
    q_scale,
    k_scale,
    v_scale,
    o_scale,
    in_gain,
    post_gain,
    q_gain,
    k_gain,
    windows,
):
    size = lax.axis_size("seq")
    chips = size // 2
    tokens, width = hidden.shape
    model_width = in_gain.shape[1]
    place = lax.axis_index("seq")
    wgt = lax.axis_index("wgt")
    core = lax.rem(place, 2)
    chip = place // 2
    pair = swap_pairs(size)
    other = [(0, 1), (1, 0)]
    in_rows = q_weight.shape[1]
    out_rows = o_weight.shape[1]
    q_share = q_weight.shape[2] // 2
    kv_share = k_weight.shape[2] // 2
    kv_heads = kv_share // HD
    reach = -(-(WINDOW - 1) // BLOCK) * BLOCK

    walk, _, _ = ring_pairs(chips)
    spots = jnp.array([walk.index(i) for i in range(chips)], jnp.int32)
    order = jnp.array(walk, jnp.int32)
    spot = spots[chip]

    def chip_at(offset):
        return order[lax.rem(spot + offset + chips, chips)]

    def factors(codes):
        return jnp.exp2(codes.astype(jnp.float32) - 127.0)

    row_block = (place * in_rows + jnp.arange(in_rows, dtype=jnp.int32)) // BLOCK
    pick = (row_block[:, None] == jnp.arange(model_width // BLOCK, dtype=jnp.int32)[None, :]).astype(jnp.float32)
    codes = [scale[layer] for layer in range(LAYERS) for scale in (q_scale, k_scale, v_scale)]
    in_factors = jnp.dot(pick, factors(jnp.concatenate(codes, axis=1)), precision=lax.Precision.HIGHEST)
    out_block = (place * out_rows + jnp.arange(out_rows, dtype=jnp.int32)) // BLOCK
    out_pick = (out_block[:, None] == jnp.arange(o_scale.shape[1], dtype=jnp.int32)[None, :]).astype(jnp.float32)
    out_codes = lax.dynamic_slice_in_dim(o_scale, wgt * (width // BLOCK), width // BLOCK, 2)
    out_factors = [
        jnp.dot(out_pick, factors(out_codes[layer]), precision=lax.Precision.HIGHEST) for layer in range(LAYERS)
    ]

    def dequantized(weight, factor, gain=None):
        rows, columns = weight.shape
        blocks = weight.reshape(rows, columns // BLOCK, BLOCK) * factor.astype(jnp.bfloat16)[:, :, None]
        if gain is not None:
            blocks = (blocks.astype(jnp.float32) * gain[:, None, None]).astype(jnp.bfloat16)
        return blocks.reshape(rows, columns)

    def split(weight):
        half = weight.shape[1] // 2
        first, second = weight[:, :half], weight[:, half:]
        return jnp.where(core == 0, first, second), jnp.where(core == 0, second, first)

    def joined(mine, theirs):
        return jnp.where(
            core == 0, jnp.concatenate([mine, theirs], axis=0), jnp.concatenate([theirs, mine], axis=0)
        )

    own_gains = lax.dynamic_slice_in_dim(in_gain, place * in_rows, in_rows, 1)
    blocks = []
    begin = 0
    for layer in range(LAYERS):
        parts = []
        for weight in (q_weight, k_weight, v_weight):
            count = weight.shape[2] // BLOCK
            factor = in_factors[:, begin : begin + count]
            parts.append(split(dequantized(weight[layer], factor, own_gains[layer])))
            begin += count
        (q_mine, q_theirs), (k_mine, k_theirs), (v_mine, v_theirs) = parts
        kv_theirs = lax.ppermute(jnp.concatenate([k_theirs, v_theirs], axis=1), "seq", pair)
        kv_block = joined(jnp.concatenate([k_mine, v_mine], axis=1), kv_theirs)
        q_block = joined(q_mine, lax.ppermute(q_theirs, "seq", pair))
        blocks += [kv_block, q_block, dequantized(o_weight[layer], out_factors[layer])]
    gathered = []
    after = None
    for number, block in enumerate(blocks):
        holds = (tuple(blocks[1:2]), tuple(blocks[2:])) if number == 0 else ()
        steps, far, after = ring_gather(block, chips, after, holds)
        gathered.append((block, steps, far))

    def own_first(own, pal):
        return jnp.concatenate([own, pal], axis=0)

    local = jnp.arange(tokens, dtype=jnp.int32)
    position = own_first(place * tokens + local, (place + 1 - 2 * core) * tokens + local)
    half = HD // 2
    inverse = rope_base ** (-jnp.arange(half, dtype=jnp.float32) * 2.0 / HD)
    angles = position.astype(jnp.float32)[:, None] * inverse[None, :]
    cosine, sine = jnp.cos(angles), jnp.sin(angles)
    cosine = jnp.concatenate([cosine, cosine], axis=1)
    sine = jnp.concatenate([-sine, sine], axis=1)
    first_key = chip * (2 * tokens) - reach

    def laid(gathered_block, rows):
        block, steps, far = gathered_block
        parts, begins = [block], [chip_at(0) * rows]
        for i, (back, ahead) in enumerate(steps):
            parts += [back, ahead]
            begins += [chip_at(-(i + 1)) * rows, chip_at(i + 1) * rows]
        farthest = chip_at(chips // 2) * rows
        parts += list(far)
        begins += [farthest, farthest + far[0].shape[0]]
        return parts, begins

    def scalars(values):
        return jnp.stack([jnp.asarray(value, jnp.int32) for value in values])

    state = hidden
    for layer in range(LAYERS):
        kv_gathered, q_gathered, o_gathered = gathered[3 * layer : 3 * layer + 3]
        far_state = lax.ppermute(state, "wgt", other)
        pal_state = lax.ppermute(state, "seq", pair)
        pal_far_state = lax.ppermute(far_state, "seq", pair)
        states = [state, far_state, pal_state, pal_far_state]
        parts, begins = laid(kv_gathered, 2 * in_rows)
        kv, factor = project(
            scalars([core, wgt] + begins),
            parts,
            states,
            cosine,
            sine,
            k_gain[layer][None, :],
            None,
            kv_heads,
            None,
            True,
        )
        pieces = [kv]
        rest = reach
        distance = 1
        while rest > 0:
            rows = min(rest, 2 * tokens)
            pairs = [(i, i + 2 * distance) for i in range(size - 2 * distance)]
            pieces.insert(0, lax.ppermute(kv[2 * tokens - rows :], "seq", pairs))
            rest -= rows
            distance += 1
        parts, begins = laid(q_gathered, 2 * in_rows)
        queries = project(
            scalars([core, wgt] + begins),
            parts,
            states,
            cosine,
            sine,
            q_gain[layer][None, :],
            factor,
            q_share // HD,
            query_scale,
            False,
        )
        mixed = attend(queries, pieces, scalars([core, first_key, windows[layer]]), reach)
        near = mixed[:tokens]
        near_pal = lax.ppermute(mixed[tokens:], "seq", pair)
        far_mixed = lax.ppermute(near, "wgt", other)
        far_pal = lax.ppermute(near_pal, "wgt", other)
        spots_of = [
            jnp.bitwise_xor(wgt, i // 2) * 2 + jnp.bitwise_xor(core, i % 2) for i in range(4)
        ]
        parts, begins = laid(o_gathered, 2 * out_rows)
        theirs = [lax.ppermute(part, "seq", pair) for part in parts]
        own_begins = [begin + core * out_rows for begin in begins]
        their_begins = [begin + (1 - core) * out_rows for begin in begins]
        projected, squares = output(
            scalars(spots_of + own_begins + their_begins), parts + theirs, [near, near_pal, far_mixed, far_pal]
        )
        squares = squares[:, 0].reshape(-1, HD)
        squares = (squares + lax.ppermute(squares, "wgt", other)).reshape(-1)
        post = projected * lax.rsqrt(squares / model_width + eps)[:, None] * post_gain[layer][None, :]
        state = (state.astype(jnp.float32) + post).astype(jnp.bfloat16)
    return state


def fits_pairs(size, wgts, shapes):
    tokens, width = shapes[0]
    return (
        wgts == 2
        and size % 4 == 0
        and tokens % 128 == 0
        and width % BLOCK == 0
        and shapes[1][2] % (2 * HD) == 0
        and shapes[2][2] % (2 * HD) == 0
        and (shapes[1][2] // 2) % shapes[4][1] == 0
        and shapes[4][1] % 32 == 0
        and shapes[1][1] % 16 == 0
        and (2 * width) % size == 0
    )


def per_device(*arrays):
    shapes = [array.shape for array in arrays]
    if fits_pairs(lax.axis_size("seq"), lax.axis_size("wgt"), shapes):
        return per_device_pairs(*arrays)
    return per_device_plain(*arrays)


def solution(mesh):
    placed = (
        P("seq", "wgt"),
        P(None, "seq", "wgt"),
        P(None, "seq", "wgt"),
        P(None, "seq", "wgt"),
        P(None, "seq", "wgt"),
        P(None, None, "wgt"),
        P(None, None, "wgt"),
        P(None, None, "wgt"),
        P(),
        P(),
        P(None, "wgt"),
        P(),
        P(),
        P(),
    )
    return jax.shard_map(
        per_device, mesh=mesh, in_specs=placed, out_specs=P("seq", "wgt"), check_vma=False
    )
```
